32 devices in a mesh: groups: 2 (over y), chol: 4 (over z), walk: 4 (over x, core).
Axes of the slice: x: 2, y: 2, z: 4, core: 2. Of those that a mesh axis runs over, the one named last changes fastest.
Arguments:
- green: bfloat16 [8, 200, 1600], P(('groups', 'walk')), parts along dimension 0, may hold values from -2 to 2
- chol: bfloat16 [16, 200, 1600], P(('groups', 'chol')), parts along dimension 0, may hold values from -0.19921875 to 0.19921875
- trial: bfloat16 [3200, 200], P(('groups', 'chol')), parts along dimension 0, may hold values from -1.1953125 to 1.1953125
- hamil: bfloat16 [1600, 1600], P('chol'), may hold values from -0.21875 to 0.21875
- energy_cot: float32 [8], P('groups'), parts along dimension 0, may hold values from -4 to 4
Outputs:
- d_green: float32 [8, 200, 1600], P(('groups', 'walk'), None, 'chol'), parts along dimension 0
- d_chol: float32 [16, 200, 1600], P(('groups', 'chol'), None, 'walk'), parts along dimension 0
- d_trial: float32 [3200, 200], P(('groups', 'chol')), parts along dimension 0
The draws below stay inside these ranges and needn't reach their ends.
There are 2 independent parts, one for each index of `groups`. The reference program is written for one: setup_inputs(seed, part) draws one part's arguments, and reference() takes and returns one part's arrays. A program takes and returns all parts, laid end to end along the dimension named above; an argument that names none is the same for every part. Nothing has to cross between parts.
All inputs are finite; a program needn't handle non-finite values.
Results may differ from the reference program's by a relative error of at most 0.0029.
Values may be sent and summed in bfloat16 or wider, within the bound.
A program may use at most 64 MiB of HBM per device.

```python
import jax
import jax.numpy as jnp
from jax import lax

NOCC = 200
NORB = 1600
NCHOL = 8
NWALK = 4


def raised(result, own_key, source, target, blocks, factor):
    owner, partner = [(jnp.arange(result.shape[position]) // (result.shape[position] // blocks)).reshape([-1 if axis == position else 1 for axis in range(result.ndim)]) for position in (source, target)]
    chosen = jax.random.permutation(own_key, blocks)[partner]
    strong = (owner == chosen) | (owner == (partner + blocks // 2) % blocks)
    return jnp.where(strong, factor * result, result)


def block_scale(rng, dims, pieces, low, largest):
    def one(position, shards_of):
        heights = jax.random.uniform(jax.random.fold_in(jax.random.fold_in(rng, 6), position), (shards_of,), jnp.float32, low / len(pieces), largest / len(pieces))
        return jnp.repeat(jnp.exp(heights), dims[position] // shards_of).reshape((-1,) + (1,) * (len(dims) - position - 1))

    level = one(*pieces[0])
    for cut in pieces[1:]:
        level = level * one(*cut)
    return level


def centred(rng, extent, deviation, limit, cuts=(), kind=jnp.bfloat16):
    array = jax.random.normal(rng, extent, jnp.float32) * deviation
    if len(cuts) > 0:
        array = block_scale(rng, extent, cuts, -0.22, 0.18) * array
    return jnp.clip(array, min=-limit, max=limit).astype(kind)


def bell_draw_with(key, shape, width, most, cuts, heavy, kind=jnp.bfloat16):
    array = width * jax.random.normal(key, shape, jnp.float32)
    if cuts:
        array = array * block_scale(key, shape, cuts, -0.22, 0.18)
    return jnp.clip(raised(array, jax.random.fold_in(key, 3), *heavy), -most, most).astype(kind)


def setup_inputs(seed: int = 0, part: int = 0) -> dict:
    key_of = jax.random.split(jax.random.key(seed), 6)
    part_splits = jax.random.split(jax.random.fold_in(key_of[5], part), 6)
    green = centred(part_splits[0], (NWALK, NOCC, NORB), 0.3, 2.0, ((0, 4),))
    chol = bell_draw_with(part_splits[1], (NCHOL, NOCC, NORB), 0.02, 0.19921875, ((0, 4),), (0, 2, 4, 2.0))
    trial = centred(part_splits[2], (NORB, NOCC), 0.2, 1.1953125, ((0, 4),))
    hamil = bell_draw_with(key_of[3], (NORB, NORB), NORB ** -0.5, 0.21875, ((0, 4),), (0, 1, 4, 2.0))
    energy_cot = centred(part_splits[4], (NWALK,), 1.0, 4.0, (), jnp.float32)
    return dict(green=green, chol=chol, trial=trial, hamil=hamil, energy_cot=energy_cot)


def reference(green, chol, trial, hamil, energy_cot):
    green_f32 = green.astype(jnp.float32)
    hrot = jnp.dot(trial.T, hamil, preferred_element_type=jnp.float32)
    identity = jnp.eye(NOCC, dtype=jnp.float32)

    def accumulate(total, slab_vec):
        slab_f32 = slab_vec.astype(jnp.float32)
        coulomb = jnp.einsum("wip,ip->w", green_f32, slab_f32)
        exchange_mat = jnp.einsum("ip,wjp->wij", slab_f32, green_f32)
        kernel_mat = (energy_cot[:, None, None] * (coulomb[:, None, None] * identity - exchange_mat)).astype(jnp.bfloat16)
        kernel_f32 = lax.optimization_barrier(kernel_mat).astype(jnp.float32)
        slab_grad = jnp.einsum("wji,wjp->ip", kernel_f32, green_f32)
        total = total + jnp.einsum("wij,jp->wip", kernel_f32, slab_f32)
        return total, slab_grad

    start_total = energy_cot[:, None, None] * hrot[None]
    d_green, d_chol = lax.scan(accumulate, start_total, chol)
    gbar = jnp.einsum("w,wip->ip", energy_cot, green_f32, precision=lax.Precision.HIGHEST).astype(jnp.bfloat16)
    d_trial = jnp.dot(hamil, gbar.T, preferred_element_type=jnp.float32)
    return d_green, d_chol, d_trial
```

```python
import functools

import jax
import jax.numpy as jnp
from jax import lax
from jax.experimental import pallas as pl
from jax.experimental.pallas import tpu as pltpu
from jax.sharding import PartitionSpec as P

MESH = pl.DeviceIdType.MESH
F32 = jnp.float32
BF16 = jnp.bfloat16


def nt(a, b):
    return lax.dot_general(a, b, (((1,), (1,)), ((), ())), preferred_element_type=F32)


def nn(a, b):
    return lax.dot_general(a, b, (((1,), (0,)), ((), ())), preferred_element_type=F32)


def tn(a, b):
    return lax.dot_general(a, b, (((0,), (0,)), ((), ())), preferred_element_type=F32)


def kernel_of(exchange, cot):
    rows = lax.broadcasted_iota(jnp.int32, exchange.shape, 0)
    cols = lax.broadcasted_iota(jnp.int32, exchange.shape, 1)
    diagonal = rows == cols
    coulomb = jnp.sum(jnp.where(diagonal, exchange, 0.0))
    return (cot * (jnp.where(diagonal, coulomb, 0.0) - exchange)).astype(BF16)


def row_chunks(rows, count):
    step = -(-rows // count) // 16 * 16
    starts = [step * k for k in range(count)]
    return [(s, (rows if k == count - 1 else s + step) - s) for k, s in enumerate(starts)]


def body(
    n_chol, chunks, cot_ref, green_ref, chol_ref, trial_ref, hamil_ref,
    dgreen_ref, dchol_ref, dtrial_ref,
    greens, part, mine, outbox, inbox, gbar, green_q,
    core_send, core_recv, x_send, x_recv, relay_send, relay_recv, z_send, z_recv,
):
    walk = lax.axis_index("walk")
    rank = lax.axis_index("chol")
    n_walk = 4
    n_vec = chol_ref.shape[0]
    peer = [walk, walk + 1 - 2 * (walk % 2), (walk + 2) % n_walk, n_walk - 1 - walk]
    quarter = dchol_ref.shape[2]
    third = dgreen_ref.shape[2]

    barrier = pltpu.get_barrier_semaphore()
    for d in (1, 2):
        pl.semaphore_signal(barrier, inc=1, device_id={"walk": peer[d]}, device_id_type=MESH)
    for c in range(1, n_chol):
        pl.semaphore_signal(
            barrier, inc=1, device_id={"chol": (rank + c) % n_chol}, device_id_type=MESH
        )
    pl.semaphore_wait(barrier, 2 + n_chol - 1)

    def to_core():
        return pltpu.make_async_remote_copy(
            green_ref.at[0], greens.at[1], core_send, core_recv,
            device_id={"walk": peer[1]}, device_id_type=MESH,
        )

    def to_x(k):
        span = pl.ds(*chunks[k])
        return pltpu.make_async_remote_copy(
            green_ref.at[0, span], greens.at[2, span], x_send.at[k], x_recv.at[k],
            device_id={"walk": peer[2]}, device_id_type=MESH,
        )

    def relay(k):
        span = pl.ds(*chunks[k])
        return pltpu.make_async_remote_copy(
            greens.at[2, span], greens.at[3, span], relay_send.at[k], relay_recv.at[k],
            device_id={"walk": peer[1]}, device_id_type=MESH,
        )

    def to_z(c):
        return pltpu.make_async_remote_copy(
            outbox.at[c], inbox.at[rank], z_send.at[c], z_recv.at[rank],
            device_id={"chol": c}, device_id_type=MESH,
        )

    def from_z(c):
        return pltpu.make_async_remote_copy(
            outbox.at[c], inbox.at[c], z_send.at[c], z_recv.at[c],
            device_id={"chol": c}, device_id_type=MESH,
        )

    for k in range(len(chunks)):
        to_x(k).start()
    to_core().start()

    cot = cot_ref[walk]
    total = cot * tn(trial_ref[...], hamil_ref[...])
    for g in range(n_vec):
        total = total + nn(kernel_of(nt(chol_ref[g], green_ref[0]), cot), chol_ref[g])
    part[...] = total
    for c in range(n_chol):
        piece = part[:, c * third:(c + 1) * third]

        @pl.when(rank == c)
        def _():
            mine[...] = piece

        @pl.when(rank != c)
        def _():
            outbox[c] = piece.astype(BF16)
            to_z(c).start()

    def absorb(d, green):
        weight = cot_ref[peer[d]]
        wide = green.astype(F32)
        if d == 0:
            gbar[...] = weight * wide
        else:
            gbar[...] += weight * wide
        for q in range(n_walk):

            @pl.when(walk == q)
            def _():
                green_q[...] = wide[:, q * quarter:(q + 1) * quarter].astype(BF16)

        for g in range(n_vec):
            term = nn(kernel_of(nt(green, chol_ref[g]), weight), green_q[...])
            if d == 0:
                dchol_ref[g] = term
            else:
                dchol_ref[g] += term

    absorb(0, green_ref[0])
    for k in range(len(chunks)):
        if k == 1:
            to_core().wait_recv()
            absorb(1, greens[1])
        to_x(k).wait_recv()
        relay(k).start()
    absorb(2, greens[2])
    for k in range(len(chunks)):
        relay(k).wait_recv()
    absorb(3, greens[3])
    dtrial_ref[...] = nt(hamil_ref[...], gbar[...].astype(BF16))

    for c in range(n_chol):

        @pl.when(rank != c)
        def _():
            from_z(c).wait_recv()
            mine[...] += inbox[c].astype(F32)

    dgreen_ref[0] = mine[...]
    to_core().wait_send()
    for k in range(len(chunks)):
        to_x(k).wait_send()
        relay(k).wait_send()
    for c in range(n_chol):

        @pl.when(rank != c)
        def _():
            to_z(c).wait_send()


def fused(green, chol, trial, hamil, energy_cot):
    n_chol = lax.axis_size("chol")
    n_walk = lax.axis_size("walk")
    _, occ, orb = green.shape
    chunks = row_chunks(occ, 3)
    vmem = pl.BlockSpec(memory_space=pltpu.VMEM)
    dma = pltpu.SemaphoreType.DMA
    return pl.pallas_call(
        functools.partial(body, n_chol, chunks),
        out_shape=(
            jax.ShapeDtypeStruct((1, occ, orb // n_chol), F32),
            jax.ShapeDtypeStruct((chol.shape[0], occ, orb // n_walk), F32),
            jax.ShapeDtypeStruct((hamil.shape[0], occ), F32),
        ),
        in_specs=[pl.BlockSpec(memory_space=pltpu.SMEM)] + [vmem] * 4,
        out_specs=(vmem,) * 3,
        scratch_shapes=[
            pltpu.VMEM((n_walk, occ, orb), BF16),
            pltpu.VMEM((occ, orb), F32),
            pltpu.VMEM((occ, orb // n_chol), F32),
            pltpu.VMEM((n_chol, occ, orb // n_chol), BF16),
            pltpu.VMEM((n_chol, occ, orb // n_chol), BF16),
            pltpu.VMEM((occ, orb), F32),
            pltpu.VMEM((occ, orb // n_walk), BF16),
            dma, dma,
            dma((len(chunks),)), dma((len(chunks),)),
            dma((len(chunks),)), dma((len(chunks),)),
            dma((n_chol,)), dma((n_chol,)),
        ],
        compiler_params=pltpu.CompilerParams(
            collective_id=0, has_side_effects=True, vmem_limit_bytes=60 * 1024 * 1024
        ),
    )(energy_cot, green, chol, trial, hamil)


def shards(green, chol, trial, hamil, energy_cot):
    walk_rank = lax.axis_index("walk")
    walk_rows = green.shape[0]
    cot_own = lax.dynamic_slice_in_dim(energy_cot, walk_rank * walk_rows, walk_rows, 0)
    hrot_part = lax.dot_general(
        trial, hamil, (((0,), (0,)), ((), ())), preferred_element_type=jnp.float32
    )
    identity = jnp.eye(trial.shape[1], dtype=jnp.float32)
    quarter = green.shape[2] // lax.axis_size("walk")
    greens = lax.all_gather(green, "walk", axis=0, tiled=True)
    coulomb = jnp.einsum("cip,wip->cw", chol, greens, preferred_element_type=jnp.float32)
    exchange_mat = jnp.einsum("cip,wjp->cwij", chol, greens, preferred_element_type=jnp.float32)
    kernel_mat = (
        energy_cot[None, :, None, None] * (coulomb[:, :, None, None] * identity - exchange_mat)
    ).astype(jnp.bfloat16)
    kernel_own = lax.dynamic_slice_in_dim(kernel_mat, walk_rank * walk_rows, walk_rows, 1)
    green_part = jnp.einsum("cwij,cjp->wip", kernel_own, chol, preferred_element_type=jnp.float32)
    green_part = green_part + cot_own[:, None, None] * hrot_part[None]
    d_green = lax.psum_scatter(green_part, "chol", scatter_dimension=2, tiled=True)
    green_share = lax.dynamic_slice_in_dim(greens, walk_rank * quarter, quarter, 2)
    d_chol = jnp.einsum(
        "cwji,wjp->cip", kernel_mat, green_share, preferred_element_type=jnp.float32
    )
    gbar = jnp.einsum(
        "w,wip->ip",
        energy_cot,
        greens,
        precision=lax.Precision.HIGHEST,
        preferred_element_type=jnp.float32,
    ).astype(jnp.bfloat16)
    d_trial = lax.dot_general(
        hamil, gbar, (((1,), (1,)), ((), ())), preferred_element_type=jnp.float32
    )
    return (d_green, d_chol, d_trial)


def solution(mesh):
    direct = mesh.shape["walk"] == 4 and mesh.shape["chol"] <= 8
    return jax.shard_map(
        fused if direct else shards,
        mesh=mesh,
        in_specs=(
            P(("groups", "walk"), None, None),
            P(("groups", "chol"), None, None),
            P(("groups", "chol"), None),
            P("chol", None),
            P("groups"),
        ),
        out_specs=(
            P(("groups", "walk"), None, "chol"),
            P(("groups", "chol"), None, "walk"),
            P(("groups", "chol"), None),
        ),
        check_vma=False,
    )
```

```python
import functools

import jax
import jax.numpy as jnp
from jax import lax
from jax.experimental import pallas as pl
from jax.experimental.pallas import tpu as pltpu
from jax.sharding import PartitionSpec as P

MESH = pl.DeviceIdType.MESH
F32 = jnp.float32
BF16 = jnp.bfloat16


def nt(a, b):
    return lax.dot_general(a, b, (((1,), (1,)), ((), ())), preferred_element_type=F32)


def nn(a, b):
    return lax.dot_general(a, b, (((1,), (0,)), ((), ())), preferred_element_type=F32)


def tn(a, b):
    return lax.dot_general(a, b, (((0,), (0,)), ((), ())), preferred_element_type=F32)


def kernel_of(exchange, cot):
    rows = lax.broadcasted_iota(jnp.int32, exchange.shape, 0)
    cols = lax.broadcasted_iota(jnp.int32, exchange.shape, 1)
    diagonal = rows == cols
    coulomb = jnp.sum(jnp.where(diagonal, exchange, 0.0))
    return (cot * (jnp.where(diagonal, coulomb, 0.0) - exchange)).astype(BF16)


def row_chunks(rows, count):
    step = -(-rows // count) // 16 * 16
    starts = [step * k for k in range(count)]
    return [(s, (rows if k == count - 1 else s + step) - s) for k, s in enumerate(starts)]


def body(
    n_chol, chunks, cot_ref, green_hbm, chol_hbm, trial_hbm, hamil_hbm,
    dgreen_ref, dchol_ref, dtrial_ref,
    green_ref, chol_ref, trial_ref, hamil_ref,
    greens, held, outbox, inbox, foldbox, gbar, green_q, kernels,
    load_sem, core_send, core_recv, x_send, x_recv, relay_send, relay_recv,
    z_send, z_recv, fold_recv,
):
    walk = lax.axis_index("walk")
    rank = lax.axis_index("chol")
    n_walk = 4
    n_vec = chol_ref.shape[0]
    peer = [walk, walk + 1 - 2 * (walk % 2), (walk + 2) % n_walk, n_walk - 1 - walk]
    quarter = dchol_ref.shape[2]
    third = dgreen_ref.shape[2]
    orb = green_ref.shape[1]
    last = n_chol - 1
    folds = {(0, last): 1, (last, 0): last - 1} if n_chol == 4 else {}

    barrier = pltpu.get_barrier_semaphore()
    for d in (1, 2):
        pl.semaphore_signal(barrier, inc=1, device_id={"walk": peer[d]}, device_id_type=MESH)
    for c in range(1, n_chol):
        pl.semaphore_signal(
            barrier, inc=1, device_id={"chol": (rank + c) % n_chol}, device_id_type=MESH
        )
    loads = [
        pltpu.make_async_copy(source, target, load_sem.at[k])
        for k, (source, target) in enumerate((
            (green_hbm.at[0], green_ref), (chol_hbm, chol_ref),
            (trial_hbm, trial_ref), (hamil_hbm, hamil_ref),
        ))
    ]
    for load in loads:
        load.start()
    pl.semaphore_wait(barrier, 2 + n_chol - 1)

    def to_core():
        return pltpu.make_async_remote_copy(
            green_hbm.at[0], greens.at[1], core_send, core_recv,
            device_id={"walk": peer[1]}, device_id_type=MESH,
        )

    def to_x(k):
        span = pl.ds(*chunks[k])
        return pltpu.make_async_remote_copy(
            green_hbm.at[0, span], greens.at[2, span], x_send.at[k], x_recv.at[k],
            device_id={"walk": peer[2]}, device_id_type=MESH,
        )

    def relay(k):
        span = pl.ds(*chunks[k])
        return pltpu.make_async_remote_copy(
            greens.at[2, span], greens.at[3, span], relay_send.at[k], relay_recv.at[k],
            device_id={"walk": peer[1]}, device_id_type=MESH,
        )

    def to_z(c):
        return pltpu.make_async_remote_copy(
            outbox.at[c], inbox.at[rank], z_send.at[c], z_recv.at[rank],
            device_id={"chol": c}, device_id_type=MESH,
        )

    def from_z(c):
        return pltpu.make_async_remote_copy(
            outbox.at[c], inbox.at[c], z_send.at[c], z_recv.at[c],
            device_id={"chol": c}, device_id_type=MESH,
        )

    def to_fold(c, middle):
        return pltpu.make_async_remote_copy(
            outbox.at[c], foldbox, z_send.at[c], fold_recv,
            device_id={"chol": middle}, device_id_type=MESH,
        )

    for k in range(len(chunks)):
        to_x(k).start()
    to_core().start()

    cot = cot_ref[walk]
    loads[0].wait()
    loads[1].wait()
    for g in range(n_vec):
        kernels[g] = kernel_of(nt(chol_ref[g], green_ref[...]), cot)
    loads[2].wait()
    loads[3].wait()
    for c in [last] + list(range(last)):
        low = c * third // 128 * 128
        high = min(orb, -(-(c + 1) * third // 128) * 128)
        window = cot * tn(trial_ref[...], hamil_ref[:, low:high])
        for g in range(n_vec):
            window = window + nn(kernels[g], chol_ref[g, :, low:high])
        piece = window[:, c * third - low:(c + 1) * third - low]
        for r in range(n_chol):

            @pl.when(rank == r)
            def _():
                if r == c:
                    dgreen_ref[0] = piece
                elif (r, c) in folds:
                    outbox[c] = piece.astype(BF16)
                    to_fold(c, folds[r, c]).start()
                elif any(end == c and folds[start, end] == r for start, end in folds):
                    held[...] = piece
                else:
                    outbox[c] = piece.astype(BF16)
                    to_z(c).start()

    def absorb(d, green):
        weight = cot_ref[peer[d]]
        wide = green.astype(F32)
        if d == 0:
            gbar[...] = weight * wide
        else:
            gbar[...] += weight * wide
        for q in range(n_walk):

            @pl.when(walk == q)
            def _():
                green_q[...] = wide[:, q * quarter:(q + 1) * quarter].astype(BF16)

        for g in range(n_vec):
            term = nn(kernel_of(nt(green, chol_ref[g]), weight), green_q[...])
            if d == 0:
                dchol_ref[g] = term
            else:
                dchol_ref[g] += term

    absorb(0, green_ref[...])
    for (start, end), middle in folds.items():

        @pl.when(rank == middle)
        def _():
            to_fold(end, middle).wait_recv()
            outbox[end] = (held[...] + foldbox[...].astype(F32)).astype(BF16)
            to_z(end).start()

    for k in range(len(chunks)):
        if k == 1:
            to_core().wait_recv()
            absorb(1, greens[1])
        to_x(k).wait_recv()
        relay(k).start()
    absorb(2, greens[2])
    for k in range(len(chunks)):
        relay(k).wait_recv()
    absorb(3, greens[3])
    dtrial_ref[...] = nt(hamil_ref[...], gbar[...].astype(BF16))

    for r in range(n_chol):

        @pl.when(rank == r)
        def _():
            for c in range(n_chol):
                if c != r and (c, r) not in folds:
                    from_z(c).wait_recv()
                    dgreen_ref[0] += inbox[c].astype(F32)

    to_core().wait_send()
    for k in range(len(chunks)):
        to_x(k).wait_send()
        relay(k).wait_send()
    for c in range(n_chol):

        @pl.when(rank != c)
        def _():
            to_z(c).wait_send()


def write_out(*refs):
    sources, targets, sem = refs[:3], refs[3:6], refs[6]
    copies = [pltpu.make_async_copy(s, t, sem.at[k]) for k, (s, t) in enumerate(zip(sources, targets))]
    for copy in copies:
        copy.start()
    for copy in copies:
        copy.wait()


def fused(green, chol, trial, hamil, energy_cot):
    n_chol = lax.axis_size("chol")
    n_walk = lax.axis_size("walk")
    _, occ, orb = green.shape
    chunks = row_chunks(occ, 3)
    vmem = pl.BlockSpec(memory_space=pltpu.VMEM)
    anywhere = pl.BlockSpec(memory_space=pl.ANY)
    dma = pltpu.SemaphoreType.DMA
    shapes = [
        (1, occ, orb // n_chol),
        (chol.shape[0], occ, orb // n_walk),
        (hamil.shape[0], occ),
    ]
    results = pl.pallas_call(
        functools.partial(body, n_chol, chunks),
        out_shape=tuple(pltpu.VMEM(shape, F32) for shape in shapes),
        in_specs=[pl.BlockSpec(memory_space=pltpu.SMEM)] + [anywhere] * 4,
        out_specs=(vmem,) * 3,
        scratch_shapes=[
            pltpu.VMEM((occ, orb), BF16),
            pltpu.VMEM(chol.shape, BF16),
            pltpu.VMEM(trial.shape, BF16),
            pltpu.VMEM(hamil.shape, BF16),
            pltpu.VMEM((n_walk, occ, orb), BF16),
            pltpu.VMEM((occ, orb // n_chol), F32),
            pltpu.VMEM((n_chol, occ, orb // n_chol), BF16),
            pltpu.VMEM((n_chol, occ, orb // n_chol), BF16),
            pltpu.VMEM((occ, orb // n_chol), BF16),
            pltpu.VMEM((occ, orb), F32),
            pltpu.VMEM((occ, orb // n_walk), BF16),
            pltpu.VMEM((chol.shape[0], occ, occ), BF16),
            dma((4,)), dma, dma,
            dma((len(chunks),)), dma((len(chunks),)),
            dma((len(chunks),)), dma((len(chunks),)),
            dma((n_chol,)), dma((n_chol,)), dma,
        ],
        compiler_params=pltpu.CompilerParams(
            collective_id=0, has_side_effects=True, vmem_limit_bytes=60 * 1024 * 1024
        ),
    )(energy_cot, green, chol, trial, hamil)
    return pl.pallas_call(
        write_out,
        out_shape=tuple(jax.ShapeDtypeStruct(shape, F32) for shape in shapes),
        in_specs=[anywhere] * 3,
        out_specs=(anywhere,) * 3,
        scratch_shapes=[dma((3,))],
        compiler_params=pltpu.CompilerParams(vmem_limit_bytes=1024 * 1024),
    )(*results)


def shards(green, chol, trial, hamil, energy_cot):
    walk_rank = lax.axis_index("walk")
    walk_rows = green.shape[0]
    cot_own = lax.dynamic_slice_in_dim(energy_cot, walk_rank * walk_rows, walk_rows, 0)
    hrot_part = lax.dot_general(
        trial, hamil, (((0,), (0,)), ((), ())), preferred_element_type=jnp.float32
    )
    identity = jnp.eye(trial.shape[1], dtype=jnp.float32)
    quarter = green.shape[2] // lax.axis_size("walk")
    greens = lax.all_gather(green, "walk", axis=0, tiled=True)
    coulomb = jnp.einsum("cip,wip->cw", chol, greens, preferred_element_type=jnp.float32)
    exchange_mat = jnp.einsum("cip,wjp->cwij", chol, greens, preferred_element_type=jnp.float32)
    kernel_mat = (
        energy_cot[None, :, None, None] * (coulomb[:, :, None, None] * identity - exchange_mat)
    ).astype(jnp.bfloat16)
    kernel_own = lax.dynamic_slice_in_dim(kernel_mat, walk_rank * walk_rows, walk_rows, 1)
    green_part = jnp.einsum("cwij,cjp->wip", kernel_own, chol, preferred_element_type=jnp.float32)
    green_part = green_part + cot_own[:, None, None] * hrot_part[None]
    d_green = lax.psum_scatter(green_part, "chol", scatter_dimension=2, tiled=True)
    green_share = lax.dynamic_slice_in_dim(greens, walk_rank * quarter, quarter, 2)
    d_chol = jnp.einsum(
        "cwji,wjp->cip", kernel_mat, green_share, preferred_element_type=jnp.float32
    )
    gbar = jnp.einsum(
        "w,wip->ip",
        energy_cot,
        greens,
        precision=lax.Precision.HIGHEST,
        preferred_element_type=jnp.float32,
    ).astype(jnp.bfloat16)
    d_trial = lax.dot_general(
        hamil, gbar, (((1,), (1,)), ((), ())), preferred_element_type=jnp.float32
    )
    return (d_green, d_chol, d_trial)


def solution(mesh):
    direct = mesh.shape["walk"] == 4 and mesh.shape["chol"] <= 8
    return jax.shard_map(
        fused if direct else shards,
        mesh=mesh,
        in_specs=(
            P(("groups", "walk"), None, None),
            P(("groups", "chol"), None, None),
            P(("groups", "chol"), None),
            P("chol", None),
            P("groups"),
        ),
        out_specs=(
            P(("groups", "walk"), None, "chol"),
            P(("groups", "chol"), None, "walk"),
            P(("groups", "chol"), None),
        ),
        check_vma=False,
    )
```

```python
import functools

import jax
import jax.numpy as jnp
from jax import lax
from jax.experimental import pallas as pl
from jax.experimental.pallas import tpu as pltpu
from jax.sharding import PartitionSpec as P

MESH = pl.DeviceIdType.MESH
F32 = jnp.float32
BF16 = jnp.bfloat16


def nt(a, b):
    return lax.dot_general(a, b, (((1,), (1,)), ((), ())), preferred_element_type=F32)


def nn(a, b):
    return lax.dot_general(a, b, (((1,), (0,)), ((), ())), preferred_element_type=F32)


def tn(a, b):
    return lax.dot_general(a, b, (((0,), (0,)), ((), ())), preferred_element_type=F32)


def kernel_of(exchange, cot):
    rows = lax.broadcasted_iota(jnp.int32, exchange.shape, 0)
    cols = lax.broadcasted_iota(jnp.int32, exchange.shape, 1)
    diagonal = rows == cols
    coulomb = jnp.sum(jnp.where(diagonal, exchange, 0.0))
    return (cot * (jnp.where(diagonal, coulomb, 0.0) - exchange)).astype(BF16)


def row_chunks(rows):
    step = -(-rows // 3) // 16 * 16
    starts = [0, step * 3 // 2 // 16 * 16, 2 * step, 2 * step + step // 2 // 16 * 16]
    return [(s, e - s) for s, e in zip(starts, starts[1:] + [rows])]


def body(
    n_chol, chunks, cot_ref, green_hbm, chol_hbm, trial_hbm, hamil_hbm,
    dgreen_ref, dchol_ref, dtrial_ref,
    green_ref, chol_ref, trial_ref, hamil_ref,
    greens, held, outbox, inbox, foldbox, gbar, green_q, kernels, partial_ex,
    load_sem, core_send, core_recv, x_send, x_recv, relay_send, relay_recv,
    z_send, z_recv, fold_recv, pair_send, pair_recv,
):
    walk = lax.axis_index("walk")
    rank = lax.axis_index("chol")
    n_walk = 4
    n_vec = chol_ref.shape[0]
    peer = [walk, walk + 1 - 2 * (walk % 2), (walk + 2) % n_walk, n_walk - 1 - walk]
    quarter = dchol_ref.shape[2]
    third = dgreen_ref.shape[2]
    orb = green_ref.shape[1]
    last = n_chol - 1
    folds = {(0, last): 1, (last, 0): last - 1} if n_chol == 4 else {}

    barrier = pltpu.get_barrier_semaphore()
    for d in (1, 2):
        pl.semaphore_signal(barrier, inc=1, device_id={"walk": peer[d]}, device_id_type=MESH)
    for c in range(1, n_chol):
        pl.semaphore_signal(
            barrier, inc=1, device_id={"chol": (rank + c) % n_chol}, device_id_type=MESH
        )
    loads = [
        pltpu.make_async_copy(source, target, load_sem.at[k])
        for k, (source, target) in enumerate((
            (green_hbm.at[0], green_ref), (chol_hbm, chol_ref),
            (trial_hbm, trial_ref), (hamil_hbm, hamil_ref),
        ))
    ]
    for load in loads:
        load.start()
    pl.semaphore_wait(barrier, 2 + n_chol - 1)

    def to_core():
        return pltpu.make_async_remote_copy(
            green_hbm.at[0], greens.at[1], core_send, core_recv,
            device_id={"walk": peer[1]}, device_id_type=MESH,
        )

    def to_x(k):
        span = pl.ds(*chunks[k])
        return pltpu.make_async_remote_copy(
            green_hbm.at[0, span], greens.at[2, span], x_send.at[k], x_recv.at[k],
            device_id={"walk": peer[2]}, device_id_type=MESH,
        )

    def relay(k):
        span = pl.ds(*chunks[k])
        return pltpu.make_async_remote_copy(
            greens.at[2, span], greens.at[3, span], relay_send.at[k], relay_recv.at[k],
            device_id={"walk": peer[1]}, device_id_type=MESH,
        )

    def to_z(c):
        return pltpu.make_async_remote_copy(
            outbox.at[c], inbox.at[rank], z_send.at[c], z_recv.at[rank],
            device_id={"chol": c}, device_id_type=MESH,
        )

    def from_z(c):
        return pltpu.make_async_remote_copy(
            outbox.at[c], inbox.at[c], z_send.at[c], z_recv.at[c],
            device_id={"chol": c}, device_id_type=MESH,
        )

    def to_fold(c, middle):
        return pltpu.make_async_remote_copy(
            outbox.at[c], foldbox, z_send.at[c], fold_recv,
            device_id={"chol": middle}, device_id_type=MESH,
        )

    def to_pair(k):
        span = pl.ds(*chunks[k])
        return pltpu.make_async_remote_copy(
            greens.at[2, span], greens.at[2, span], pair_send, pair_recv,
            device_id={"chol": rank + 1 - 2 * (rank % 2)}, device_id_type=MESH,
        )

    for parity in range(2):

        @pl.when(rank % 2 == parity)
        def _():
            to_x(2 + parity).start()

    for k in range(2):
        to_x(k).start()
    to_core().start()

    cot = cot_ref[walk]
    loads[0].wait()
    loads[1].wait()
    for g in range(n_vec):
        kernels[g] = kernel_of(nt(chol_ref[g], green_ref[...]), cot)
    loads[2].wait()
    loads[3].wait()
    for turn, c in enumerate([last] + list(range(last))):
        if turn == 2:
            for parity in range(2):

                @pl.when(rank % 2 == parity)
                def _():
                    to_x(2 + parity).wait_recv()
                    to_pair(2 + parity).start()
                    relay(2 + parity).start()

        low = c * third // 128 * 128
        high = min(orb, -(-(c + 1) * third // 128) * 128)
        window = cot * tn(trial_ref[...], hamil_ref[:, low:high])
        for g in range(n_vec):
            window = window + nn(kernels[g], chol_ref[g, :, low:high])
        piece = window[:, c * third - low:(c + 1) * third - low]
        for r in range(n_chol):

            @pl.when(rank == r)
            def _():
                if r == c:
                    dgreen_ref[0] = piece
                elif (r, c) in folds:
                    outbox[c] = piece.astype(BF16)
                    to_fold(c, folds[r, c]).start()
                elif any(end == c and folds[start, end] == r for start, end in folds):
                    held[...] = piece
                else:
                    outbox[c] = piece.astype(BF16)
                    to_z(c).start()

    def absorb_rows(d, green, rows):
        weight = cot_ref[peer[d]]
        wide = green.astype(F32)
        if d == 0:
            gbar[rows, :] = weight * wide
        else:
            gbar[rows, :] += weight * wide
        for q in range(n_walk):

            @pl.when(walk == q)
            def _():
                green_q[d % 2, rows, :] = wide[:, q * quarter:(q + 1) * quarter].astype(BF16)

        for g in range(n_vec):
            partial_ex[d % 2, g, rows, :] = nt(green, chol_ref[g])

    def finish(d):
        for g in range(n_vec):
            term = nn(kernel_of(partial_ex[d % 2, g], cot_ref[peer[d]]), green_q[d % 2])
            if d == 0:
                dchol_ref[g] = term
            else:
                dchol_ref[g] += term

    def trial_columns(low, high):
        dtrial_ref[:, low:high] = nt(hamil_ref[...], gbar[low:high, :].astype(BF16))

    every = pl.ds(0, green_ref.shape[0])
    absorb_rows(0, green_ref[...], every)
    finish(0)
    for (start, end), middle in folds.items():

        @pl.when(rank == middle)
        def _():
            to_fold(end, middle).wait_recv()
            outbox[end] = (held[...] + foldbox[...].astype(F32)).astype(BF16)
            to_z(end).start()

    to_core().wait_recv()
    absorb_rows(1, greens[1], every)
    finish(1)
    split = chunks[2][0]
    rows = green_ref.shape[0]
    rest = pl.ds(split, rows - split)
    for parity in range(2):

        @pl.when(rank % 2 == parity)
        def _():
            to_pair(3 - parity).wait_recv()
            relay(3 - parity).start()

    absorb_rows(2, greens[2, rest], rest)
    relay(2).wait_recv()
    relay(3).wait_recv()
    absorb_rows(3, greens[3, rest], rest)
    trial_columns(split, rows)
    for k in range(2):
        span = pl.ds(*chunks[k])
        to_x(k).wait_recv()
        relay(k).start()
        absorb_rows(2, greens[2, span], span)
        if k == 1:
            finish(2)
        relay(k).wait_recv()
        absorb_rows(3, greens[3, span], span)
    finish(3)
    trial_columns(0, split)

    for r in range(n_chol):

        @pl.when(rank == r)
        def _():
            for c in range(n_chol):
                if c != r and (c, r) not in folds:
                    from_z(c).wait_recv()
                    dgreen_ref[0] += inbox[c].astype(F32)

    to_core().wait_send()
    for k in range(len(chunks)):
        relay(k).wait_send()
    for k in range(2):
        to_x(k).wait_send()
    for parity in range(2):

        @pl.when(rank % 2 == parity)
        def _():
            to_x(2 + parity).wait_send()
            to_pair(2 + parity).wait_send()

    for c in range(n_chol):

        @pl.when(rank != c)
        def _():
            to_z(c).wait_send()


def write_out(*refs):
    sources, targets, sem = refs[:3], refs[3:6], refs[6]
    copies = [pltpu.make_async_copy(s, t, sem.at[k]) for k, (s, t) in enumerate(zip(sources, targets))]
    for copy in copies:
        copy.start()
    for copy in copies:
        copy.wait()


def fused(green, chol, trial, hamil, energy_cot):
    n_chol = lax.axis_size("chol")
    n_walk = lax.axis_size("walk")
    _, occ, orb = green.shape
    chunks = row_chunks(occ)
    vmem = pl.BlockSpec(memory_space=pltpu.VMEM)
    anywhere = pl.BlockSpec(memory_space=pl.ANY)
    dma = pltpu.SemaphoreType.DMA
    shapes = [
        (1, occ, orb // n_chol),
        (chol.shape[0], occ, orb // n_walk),
        (hamil.shape[0], occ),
    ]
    results = pl.pallas_call(
        functools.partial(body, n_chol, chunks),
        out_shape=tuple(pltpu.VMEM(shape, F32) for shape in shapes),
        in_specs=[pl.BlockSpec(memory_space=pltpu.SMEM)] + [anywhere] * 4,
        out_specs=(vmem,) * 3,
        scratch_shapes=[
            pltpu.VMEM((occ, orb), BF16),
            pltpu.VMEM(chol.shape, BF16),
            pltpu.VMEM(trial.shape, BF16),
            pltpu.VMEM(hamil.shape, BF16),
            pltpu.VMEM((n_walk, occ, orb), BF16),
            pltpu.VMEM((occ, orb // n_chol), F32),
            pltpu.VMEM((n_chol, occ, orb // n_chol), BF16),
            pltpu.VMEM((n_chol, occ, orb // n_chol), BF16),
            pltpu.VMEM((occ, orb // n_chol), BF16),
            pltpu.VMEM((occ, orb), F32),
            pltpu.VMEM((2, occ, orb // n_walk), BF16),
            pltpu.VMEM((chol.shape[0], occ, occ), BF16),
            pltpu.VMEM((2, chol.shape[0], occ, occ), F32),
            dma((4,)), dma, dma,
            dma((len(chunks),)), dma((len(chunks),)),
            dma((len(chunks),)), dma((len(chunks),)),
            dma((n_chol,)), dma((n_chol,)), dma, dma, dma,
        ],
        compiler_params=pltpu.CompilerParams(
            collective_id=0, has_side_effects=True, vmem_limit_bytes=60 * 1024 * 1024
        ),
    )(energy_cot, green, chol, trial, hamil)
    return pl.pallas_call(
        write_out,
        out_shape=tuple(jax.ShapeDtypeStruct(shape, F32) for shape in shapes),
        in_specs=[anywhere] * 3,
        out_specs=(anywhere,) * 3,
        scratch_shapes=[dma((3,))],
        compiler_params=pltpu.CompilerParams(vmem_limit_bytes=1024 * 1024),
    )(*results)


def shards(green, chol, trial, hamil, energy_cot):
    walk_rank = lax.axis_index("walk")
    walk_rows = green.shape[0]
    cot_own = lax.dynamic_slice_in_dim(energy_cot, walk_rank * walk_rows, walk_rows, 0)
    hrot_part = lax.dot_general(
        trial, hamil, (((0,), (0,)), ((), ())), preferred_element_type=jnp.float32
    )
    identity = jnp.eye(trial.shape[1], dtype=jnp.float32)
    quarter = green.shape[2] // lax.axis_size("walk")
    greens = lax.all_gather(green, "walk", axis=0, tiled=True)
    coulomb = jnp.einsum("cip,wip->cw", chol, greens, preferred_element_type=jnp.float32)
    exchange_mat = jnp.einsum("cip,wjp->cwij", chol, greens, preferred_element_type=jnp.float32)
    kernel_mat = (
        energy_cot[None, :, None, None] * (coulomb[:, :, None, None] * identity - exchange_mat)
    ).astype(jnp.bfloat16)
    kernel_own = lax.dynamic_slice_in_dim(kernel_mat, walk_rank * walk_rows, walk_rows, 1)
    green_part = jnp.einsum("cwij,cjp->wip", kernel_own, chol, preferred_element_type=jnp.float32)
    green_part = green_part + cot_own[:, None, None] * hrot_part[None]
    d_green = lax.psum_scatter(green_part, "chol", scatter_dimension=2, tiled=True)
    green_share = lax.dynamic_slice_in_dim(greens, walk_rank * quarter, quarter, 2)
    d_chol = jnp.einsum(
        "cwji,wjp->cip", kernel_mat, green_share, preferred_element_type=jnp.float32
    )
    gbar = jnp.einsum(
        "w,wip->ip",
        energy_cot,
        greens,
        precision=lax.Precision.HIGHEST,
        preferred_element_type=jnp.float32,
    ).astype(jnp.bfloat16)
    d_trial = lax.dot_general(
        hamil, gbar, (((1,), (1,)), ((), ())), preferred_element_type=jnp.float32
    )
    return (d_green, d_chol, d_trial)


def solution(mesh):
    direct = mesh.shape["walk"] == 4 and mesh.shape["chol"] in (2, 4, 6, 8)
    return jax.shard_map(
        fused if direct else shards,
        mesh=mesh,
        in_specs=(
            P(("groups", "walk"), None, None),
            P(("groups", "chol"), None, None),
            P(("groups", "chol"), None),
            P("chol", None),
            P("groups"),
        ),
        out_specs=(
            P(("groups", "walk"), None, "chol"),
            P(("groups", "chol"), None, "walk"),
            P(("groups", "chol"), None),
        ),
        check_vma=False,
    )
```

```python
import functools

import jax
import jax.numpy as jnp
from jax import lax
from jax.experimental import pallas as pl
from jax.experimental.pallas import tpu as pltpu
from jax.sharding import PartitionSpec as P

MESH = pl.DeviceIdType.MESH
F32 = jnp.float32
BF16 = jnp.bfloat16


def nt(a, b):
    return lax.dot_general(a, b, (((1,), (1,)), ((), ())), preferred_element_type=F32)


def nn(a, b):
    return lax.dot_general(a, b, (((1,), (0,)), ((), ())), preferred_element_type=F32)


def tn(a, b):
    return lax.dot_general(a, b, (((0,), (0,)), ((), ())), preferred_element_type=F32)


def kernel_of(exchange, cot):
    rows = lax.broadcasted_iota(jnp.int32, exchange.shape, 0)
    cols = lax.broadcasted_iota(jnp.int32, exchange.shape, 1)
    diagonal = rows == cols
    coulomb = jnp.sum(jnp.where(diagonal, exchange, 0.0))
    return (cot * (jnp.where(diagonal, coulomb, 0.0) - exchange)).astype(BF16)


def row_chunks(rows):
    step = -(-rows // 3) // 16 * 16
    starts = [0, step * 3 // 2 // 16 * 16, 2 * step, 2 * step + step // 2 // 16 * 16]
    return [(s, e - s) for s, e in zip(starts, starts[1:] + [rows])]


def body(
    n_chol, chunks, cot_ref, green_hbm, chol_hbm, trial_hbm, hamil_hbm,
    dgreen_ref, dchol_ref, dtrial_ref,
    green_ref, chol_ref, trial_ref, hamil_ref,
    greens, held, outbox, inbox, foldbox, gbar, green_q, kernels, partial_ex,
    load_sem, core_send, core_recv, x_send, x_recv, relay_send, relay_recv,
    z_send, z_recv, fold_recv, pair_send, pair_recv,
):
    walk = lax.axis_index("walk")
    rank = lax.axis_index("chol")
    n_walk = 4
    n_vec = chol_ref.shape[0]
    peer = [walk, walk + 1 - 2 * (walk % 2), (walk + 2) % n_walk, n_walk - 1 - walk]
    quarter = dchol_ref.shape[2]
    third = dgreen_ref.shape[2]
    orb = green_ref.shape[1]
    last = n_chol - 1
    folds = {(0, last): 1, (last, 0): last - 1} if n_chol == 4 else {}

    barrier = pltpu.get_barrier_semaphore()
    for d in (1, 2):
        pl.semaphore_signal(barrier, inc=1, device_id={"walk": peer[d]}, device_id_type=MESH)
    for c in range(1, n_chol):
        pl.semaphore_signal(
            barrier, inc=1, device_id={"chol": (rank + c) % n_chol}, device_id_type=MESH
        )
    loads = [
        pltpu.make_async_copy(source, target, load_sem.at[k])
        for k, (source, target) in enumerate((
            (green_hbm.at[0], green_ref), (chol_hbm, chol_ref),
            (trial_hbm, trial_ref), (hamil_hbm, hamil_ref),
        ))
    ]
    for load in loads:
        load.start()
    pl.semaphore_wait(barrier, 2 + n_chol - 1)

    def to_core():
        return pltpu.make_async_remote_copy(
            green_ref, greens.at[1], core_send, core_recv,
            device_id={"walk": peer[1]}, device_id_type=MESH,
        )

    def to_x(k):
        span = pl.ds(*chunks[k])
        return pltpu.make_async_remote_copy(
            green_ref.at[span], greens.at[2, span], x_send.at[k], x_recv.at[k],
            device_id={"walk": peer[2]}, device_id_type=MESH,
        )

    def relay(k):
        span = pl.ds(*chunks[k])
        return pltpu.make_async_remote_copy(
            greens.at[2, span], greens.at[3, span], relay_send.at[k], relay_recv.at[k],
            device_id={"walk": peer[1]}, device_id_type=MESH,
        )

    def to_z(c):
        return pltpu.make_async_remote_copy(
            outbox.at[c], inbox.at[rank], z_send.at[c], z_recv.at[rank],
            device_id={"chol": c}, device_id_type=MESH,
        )

    def from_z(c):
        return pltpu.make_async_remote_copy(
            outbox.at[c], inbox.at[c], z_send.at[c], z_recv.at[c],
            device_id={"chol": c}, device_id_type=MESH,
        )

    def to_fold(c, middle):
        return pltpu.make_async_remote_copy(
            outbox.at[c], foldbox, z_send.at[c], fold_recv,
            device_id={"chol": middle}, device_id_type=MESH,
        )

    def to_pair(k):
        span = pl.ds(*chunks[k])
        return pltpu.make_async_remote_copy(
            greens.at[2, span], greens.at[2, span], pair_send, pair_recv,
            device_id={"chol": rank + 1 - 2 * (rank % 2)}, device_id_type=MESH,
        )

    loads[0].wait()
    for parity in range(2):

        @pl.when(rank % 2 == parity)
        def _():
            to_x(2 + parity).start()

    for k in range(2):
        to_x(k).start()
    to_core().start()

    cot = cot_ref[walk]
    loads[1].wait()
    for g in range(n_vec):
        kernels[g] = kernel_of(nt(chol_ref[g], green_ref[...]), cot)
    loads[2].wait()
    loads[3].wait()
    for turn, c in enumerate([last] + list(range(last))):
        if turn == 2:
            for parity in range(2):

                @pl.when(rank % 2 == parity)
                def _():
                    to_x(2 + parity).wait_recv()
                    to_pair(2 + parity).start()
                    relay(2 + parity).start()

        low = c * third // 128 * 128
        high = min(orb, -(-(c + 1) * third // 128) * 128)
        window = cot * tn(trial_ref[...], hamil_ref[:, low:high])
        for g in range(n_vec):
            window = window + nn(kernels[g], chol_ref[g, :, low:high])
        piece = window[:, c * third - low:(c + 1) * third - low]
        for r in range(n_chol):

            @pl.when(rank == r)
            def _():
                if r == c:
                    dgreen_ref[0] = piece
                elif (r, c) in folds:
                    outbox[c] = piece.astype(BF16)
                    to_fold(c, folds[r, c]).start()
                elif any(end == c and folds[start, end] == r for start, end in folds):
                    held[...] = piece
                else:
                    outbox[c] = piece.astype(BF16)
                    to_z(c).start()

    def absorb_rows(d, green, rows):
        weight = cot_ref[peer[d]]
        wide = green.astype(F32)
        if d == 0:
            gbar[rows, :] = weight * wide
        else:
            gbar[rows, :] += weight * wide
        for q in range(n_walk):

            @pl.when(walk == q)
            def _():
                green_q[d % 2, rows, :] = wide[:, q * quarter:(q + 1) * quarter].astype(BF16)

        for g in range(n_vec):
            partial_ex[d % 2, g, rows, :] = nt(green, chol_ref[g])

    def finish(d):
        for g in range(n_vec):
            term = nn(kernel_of(partial_ex[d % 2, g], cot_ref[peer[d]]), green_q[d % 2])
            if d == 0:
                dchol_ref[g] = term
            else:
                dchol_ref[g] += term

    def trial_columns(low, high):
        dtrial_ref[:, low:high] = nt(hamil_ref[...], gbar[low:high, :].astype(BF16))

    every = pl.ds(0, green_ref.shape[0])
    absorb_rows(0, green_ref[...], every)
    finish(0)
    for (start, end), middle in folds.items():

        @pl.when(rank == middle)
        def _():
            to_fold(end, middle).wait_recv()
            outbox[end] = (held[...] + foldbox[...].astype(F32)).astype(BF16)
            to_z(end).start()

    to_core().wait_recv()
    absorb_rows(1, greens[1], every)
    finish(1)
    split = chunks[2][0]
    rows = green_ref.shape[0]
    rest = pl.ds(split, rows - split)
    for parity in range(2):

        @pl.when(rank % 2 == parity)
        def _():
            to_pair(3 - parity).wait_recv()
            relay(3 - parity).start()

    absorb_rows(2, greens[2, rest], rest)
    relay(2).wait_recv()
    relay(3).wait_recv()
    absorb_rows(3, greens[3, rest], rest)
    trial_columns(split, rows)
    for k in range(2):
        span = pl.ds(*chunks[k])
        to_x(k).wait_recv()
        relay(k).start()
        absorb_rows(2, greens[2, span], span)
        if k == 1:
            finish(2)
        relay(k).wait_recv()
        absorb_rows(3, greens[3, span], span)
    finish(3)
    trial_columns(0, split)

    for r in range(n_chol):

        @pl.when(rank == r)
        def _():
            for c in range(n_chol):
                if c != r and (c, r) not in folds:
                    from_z(c).wait_recv()
                    dgreen_ref[0] += inbox[c].astype(F32)

    to_core().wait_send()
    for k in range(len(chunks)):
        relay(k).wait_send()
    for k in range(2):
        to_x(k).wait_send()
    for parity in range(2):

        @pl.when(rank % 2 == parity)
        def _():
            to_x(2 + parity).wait_send()
            to_pair(2 + parity).wait_send()

    for c in range(n_chol):

        @pl.when(rank != c)
        def _():
            to_z(c).wait_send()


def write_out(*refs):
    sources, targets, sem = refs[:3], refs[3:6], refs[6]
    copies = [pltpu.make_async_copy(s, t, sem.at[k]) for k, (s, t) in enumerate(zip(sources, targets))]
    for copy in copies:
        copy.start()
    for copy in copies:
        copy.wait()


def fused(green, chol, trial, hamil, energy_cot):
    n_chol = lax.axis_size("chol")
    n_walk = lax.axis_size("walk")
    _, occ, orb = green.shape
    chunks = row_chunks(occ)
    vmem = pl.BlockSpec(memory_space=pltpu.VMEM)
    anywhere = pl.BlockSpec(memory_space=pl.ANY)
    dma = pltpu.SemaphoreType.DMA
    shapes = [
        (1, occ, orb // n_chol),
        (chol.shape[0], occ, orb // n_walk),
        (hamil.shape[0], occ),
    ]
    results = pl.pallas_call(
        functools.partial(body, n_chol, chunks),
        out_shape=tuple(pltpu.VMEM(shape, F32) for shape in shapes),
        in_specs=[pl.BlockSpec(memory_space=pltpu.SMEM)] + [anywhere] * 4,
        out_specs=(vmem,) * 3,
        scratch_shapes=[
            pltpu.VMEM((occ, orb), BF16),
            pltpu.VMEM(chol.shape, BF16),
            pltpu.VMEM(trial.shape, BF16),
            pltpu.VMEM(hamil.shape, BF16),
            pltpu.VMEM((n_walk, occ, orb), BF16),
            pltpu.VMEM((occ, orb // n_chol), F32),
            pltpu.VMEM((n_chol, occ, orb // n_chol), BF16),
            pltpu.VMEM((n_chol, occ, orb // n_chol), BF16),
            pltpu.VMEM((occ, orb // n_chol), BF16),
            pltpu.VMEM((occ, orb), F32),
            pltpu.VMEM((2, occ, orb // n_walk), BF16),
            pltpu.VMEM((chol.shape[0], occ, occ), BF16),
            pltpu.VMEM((2, chol.shape[0], occ, occ), F32),
            dma((4,)), dma, dma,
            dma((len(chunks),)), dma((len(chunks),)),
            dma((len(chunks),)), dma((len(chunks),)),
            dma((n_chol,)), dma((n_chol,)), dma, dma, dma,
        ],
        compiler_params=pltpu.CompilerParams(
            collective_id=0, has_side_effects=True, vmem_limit_bytes=60 * 1024 * 1024
        ),
    )(energy_cot, green, chol, trial, hamil)
    return pl.pallas_call(
        write_out,
        out_shape=tuple(jax.ShapeDtypeStruct(shape, F32) for shape in shapes),
        in_specs=[anywhere] * 3,
        out_specs=(anywhere,) * 3,
        scratch_shapes=[dma((3,))],
        compiler_params=pltpu.CompilerParams(vmem_limit_bytes=1024 * 1024),
    )(*results)


def shards(green, chol, trial, hamil, energy_cot):
    walk_rank = lax.axis_index("walk")
    walk_rows = green.shape[0]
    cot_own = lax.dynamic_slice_in_dim(energy_cot, walk_rank * walk_rows, walk_rows, 0)
    hrot_part = lax.dot_general(
        trial, hamil, (((0,), (0,)), ((), ())), preferred_element_type=jnp.float32
    )
    identity = jnp.eye(trial.shape[1], dtype=jnp.float32)
    quarter = green.shape[2] // lax.axis_size("walk")
    greens = lax.all_gather(green, "walk", axis=0, tiled=True)
    coulomb = jnp.einsum("cip,wip->cw", chol, greens, preferred_element_type=jnp.float32)
    exchange_mat = jnp.einsum("cip,wjp->cwij", chol, greens, preferred_element_type=jnp.float32)
    kernel_mat = (
        energy_cot[None, :, None, None] * (coulomb[:, :, None, None] * identity - exchange_mat)
    ).astype(jnp.bfloat16)
    kernel_own = lax.dynamic_slice_in_dim(kernel_mat, walk_rank * walk_rows, walk_rows, 1)
    green_part = jnp.einsum("cwij,cjp->wip", kernel_own, chol, preferred_element_type=jnp.float32)
    green_part = green_part + cot_own[:, None, None] * hrot_part[None]
    d_green = lax.psum_scatter(green_part, "chol", scatter_dimension=2, tiled=True)
    green_share = lax.dynamic_slice_in_dim(greens, walk_rank * quarter, quarter, 2)
    d_chol = jnp.einsum(
        "cwji,wjp->cip", kernel_mat, green_share, preferred_element_type=jnp.float32
    )
    gbar = jnp.einsum(
        "w,wip->ip",
        energy_cot,
        greens,
        precision=lax.Precision.HIGHEST,
        preferred_element_type=jnp.float32,
    ).astype(jnp.bfloat16)
    d_trial = lax.dot_general(
        hamil, gbar, (((1,), (1,)), ((), ())), preferred_element_type=jnp.float32
    )
    return (d_green, d_chol, d_trial)


def solution(mesh):
    direct = mesh.shape["walk"] == 4 and mesh.shape["chol"] in (2, 4, 6, 8)
    return jax.shard_map(
        fused if direct else shards,
        mesh=mesh,
        in_specs=(
            P(("groups", "walk"), None, None),
            P(("groups", "chol"), None, None),
            P(("groups", "chol"), None),
            P("chol", None),
            P("groups"),
        ),
        out_specs=(
            P(("groups", "walk"), None, "chol"),
            P(("groups", "chol"), None, "walk"),
            P(("groups", "chol"), None),
        ),
        check_vma=False,
    )
```
